512 devices in a mesh: dp: 8 (over y, core), expert: 64 (over z, x).
Axes of the slice: x: 4, y: 4, z: 16, core: 2. Of those that a mesh axis runs over, the one named last changes fastest.
Arguments:
- tokens: bfloat16 [65536, 1024], P(('dp', 'expert')), may hold values from -6 to 6
- cotangent: bfloat16 [65536, 1024], P(('dp', 'expert')), may hold values from -6 to 6
- expert_ids: int32 [65536, 2], P(('dp', 'expert')), may hold values from 0 to 31, all different within a row; in each aligned block of 128 rows (0 to 127, 128 to 255, ...) at most 10 rows name the same one
- gates: float32 [65536, 2], P(('dp', 'expert')), may hold values from 0.25 to 1
- expert_home: int32 [32], replicated, may hold values from 0 to 31, each once
- up_weight: bfloat16 [64, 1024, 768], P('expert'), as said below
- down_weight: bfloat16 [64, 768, 1024], P('expert'), as said below
Outputs:
- layer_out: bfloat16 [65536, 1024], P(('dp', 'expert'))
- grad_tokens: bfloat16 [65536, 1024], P(('dp', 'expert'))
- grad_up: bfloat16 [64, 1024, 768], P('expert', 'dp')
- grad_down: bfloat16 [64, 768, 1024], P('expert', None, 'dp')
The draws below stay inside these ranges and needn't reach their ends.
Inputs may be any that keep to these rules, and one draw needn't show every extreme that they name: `expert_ids`: each row names 2 different experts. Among the 128 rows of one device (aligned blocks of 128 rows) no expert is named more than 10 times, a bound that some block reaches. A permutation: expert e has copies in slots expert_home[e] and expert_home[e] + 32. `up_weight`: slots s and s + 32 hold equal weights. `down_weight`: slots s and s + 32 hold equal weights.
All inputs are finite; a program needn't handle non-finite values.
Results may differ from the reference program's by a relative error of at most 0.015.
Values may be sent and summed in bfloat16 or wider, within the bound.
A program may use at most 64 MiB of HBM per device.

```python
import math
import jax
import jax.numpy as jnp
import numpy as np
from jax import lax

D = 1024
H = 768
TOP = 2
TOK_DEV = 128
EXPERTS = 32
CAP = 10
TOKENS = 65536
N_DP = 8
N_EXPERT = 64


def draw_up_weight(key, part):
    base = jax.random.normal(key, (EXPERTS, D, H), jnp.float32)
    base = base * (1.0 / math.sqrt(D))
    return jnp.concatenate([base, base], axis=0).astype(jnp.bfloat16)


def draw_down_weight(key, part):
    base = jax.random.normal(key, (EXPERTS, H, D), jnp.float32)
    base = base * (1.0 / math.sqrt(H))
    return jnp.concatenate([base, base], axis=0).astype(jnp.bfloat16)


def block_levels(own_key, dims, split, low, top_value):
    loudness, own = 1.0, jax.random.fold_in(own_key, 6)
    for dim, blocks in split:
        steps = jnp.exp(jax.random.uniform(jax.random.fold_in(own, dim), (blocks,), jnp.float32, low / len(split), top_value / len(split)))
        loudness = loudness * jnp.repeat(steps, dims[dim] // blocks).reshape([-1 if axis == dim else 1 for axis in range(len(dims))])
    return loudness


def assign_block(stream_key, own, number, rows, amount, top, reach, slope):
    ranking = jax.random.permutation(stream_key, amount)
    crowded, common = load_shares(amount, rows * top, reach, slope, True), load_shares(amount, rows * top, reach, slope, False)
    places = jnp.arange(amount)

    def named(sizes, offset_by):
        used = int((sizes > 0).sum())
        fixed = max(1, used // 4)
        passed = fixed + (places - fixed + offset_by * (used - fixed)) % max(1, amount - fixed)
        return jnp.zeros((amount,), jnp.int32).at[ranking[jnp.where(places < fixed, places, passed)]].set(jnp.asarray(sizes, jnp.int32))

    sizes = jnp.where(number % 4 == 0, named(crowded, number // 4), named(common, number - number // 4 - 1))
    mixed = jax.random.permutation(jax.random.fold_in(own, 3), amount)
    donor, receiver = mixed[0:amount // 2 * 2:2], mixed[1:amount // 2 * 2:2]
    room = jnp.minimum(sizes[donor] - 1, reach - sizes[receiver]) // 2
    room = jnp.where((donor == ranking[0]) | (receiver == ranking[0]) | (sizes[receiver] == 0), 0, jnp.maximum(room, 0))
    passed = jax.random.randint(jax.random.fold_in(own, 4), (amount // 2,), 0, 1 << 20) % (room + 1)
    sizes = sizes.at[donor].add(-passed).at[receiver].add(passed)
    members = jnp.searchsorted(jnp.cumsum(sizes), jnp.arange(rows * top), side="right").astype(jnp.int32)
    grid = members.reshape(top, rows).T
    grid = grid[jax.random.permutation(jax.random.fold_in(own, 1), rows)]
    offset_by = jax.random.randint(jax.random.fold_in(own, 2), (rows, 1), 0, top)
    return jnp.take_along_axis(grid, (jnp.arange(top)[None, :] + offset_by) % top, axis=1)


def load_shares(count, total, reach, skew, full):
    portions = [(1 << 20) // math.isqrt(standing ** skew) + 1 for standing in range(1, count + 1)]
    largest = reach if full else min(reach, max(-(-total // count), total * portions[0] // sum(portions)))
    least = 1 if total - largest >= count - 1 else 0
    given, rest = [largest] + [least] * (count - 1), total - largest - least * (count - 1)
    while rest > 0:
        movable = [i for i in range(1, count) if given[i] < largest] or [i for i in range(1, count) if given[i] < reach]
        pool, budget = sum([portions[i] for i in movable]), rest
        for i in movable:
            extra = min(reach - given[i], max(1, budget * portions[i] // pool), rest)
            given[i] = given[i] + extra
            rest = rest - extra
    return np.array(given)


def noise(rng, extent, spread, limit, cuts=(), kind=jnp.bfloat16):
    array = spread * jax.random.normal(rng, extent, jnp.float32)
    if cuts:
        array = array * block_levels(rng, extent, cuts, -0.22, 0.18)
    return jnp.clip(array, -limit, limit).astype(kind)


def setup_inputs(seed: int = 0) -> dict:
    streams_of = jax.random.split(jax.random.key(seed), 8)
    tokens = noise(streams_of[0], (TOKENS, D), 1.0, 6.0, ((0, 512),))
    cotangent = noise(streams_of[1], (TOKENS, D), 1.0, 6.0, ((0, 512),))
    expert_ids_keys = jax.random.split(jax.random.fold_in(streams_of[2], 1), TOKENS // TOK_DEV)
    expert_ids_turns = jax.random.permutation(jax.random.fold_in(streams_of[2], 3), TOKENS // TOK_DEV)
    expert_ids = jax.vmap(lambda own, number: assign_block(jax.random.fold_in(streams_of[2], 2), own, number, TOK_DEV, EXPERTS, TOP, CAP, 2))(expert_ids_keys, expert_ids_turns).reshape((TOKENS, TOP))
    gates = jnp.clip(0.25 + 0.75 * jax.random.uniform(streams_of[3], (TOKENS, TOP), jnp.float32) ** block_levels(streams_of[3], (TOKENS, TOP), ((0, 512),), -0.2, 0.2), 0.25, 1.0)
    expert_home = jax.random.permutation(streams_of[4], EXPERTS).astype(jnp.int32)
    up_weight = draw_up_weight(jax.random.fold_in(streams_of[7], 71), 0)
    down_weight = draw_down_weight(jax.random.fold_in(streams_of[7], 71), 0)
    return {"tokens": tokens, "cotangent": cotangent, "expert_ids": expert_ids, "gates": gates, "expert_home": expert_home, "up_weight": up_weight, "down_weight": down_weight}


def silu_grad(hidden_in):
    sigmoid = jax.nn.sigmoid(hidden_in)
    return sigmoid * (1.0 + hidden_in * (1.0 - sigmoid))

def reference(tokens, cotangent, expert_ids, gates, expert_home, up_weight, down_weight):
    group_tokens = TOK_DEV * N_EXPERT
    pair_total = group_tokens * TOP
    bound = N_EXPERT * CAP
    expert_range = jnp.arange(EXPERTS, dtype=jnp.int32)
    tokens_group = tokens.reshape(N_DP, group_tokens, D)
    cot_group = cotangent.reshape(N_DP, group_tokens, D)
    ids_group = expert_ids.reshape(N_DP, pair_total).astype(jnp.int32)
    gates_group = gates.reshape(N_DP, pair_total)

    def group_step(carry, inputs):
        sum_up, sum_down = carry
        group_x, group_dy, group_ids, group_gates = inputs
        ordering = jnp.argsort(group_ids, stable=True).astype(jnp.int32)
        counted = lax.optimization_barrier(jnp.sum((group_ids[:, None] == expert_range[None, :]).astype(jnp.int32), axis=0))
        begins = (jnp.cumsum(counted) - counted).astype(jnp.int32)

        def per_expert(expert_num):
            offsets = jnp.arange(bound, dtype=jnp.int32)
            filled = offsets < counted[expert_num]
            position = jnp.clip(begins[expert_num] + offsets, 0, pair_total - 1).astype(jnp.int32)
            pair_index = jnp.where(filled, ordering[position], 0).astype(jnp.int32)
            token_index = (pair_index // TOP).astype(jnp.int32)
            in_rows = jnp.where(filled[:, None], group_x[token_index], jnp.zeros((), jnp.bfloat16))
            gate_value = jnp.where(filled, group_gates[pair_index], 0.0)
            dy_rows = (gate_value[:, None] * group_dy[token_index].astype(jnp.float32)).astype(jnp.bfloat16)
            slot = expert_home[expert_num]
            weight_up = up_weight[slot]
            weight_down = down_weight[slot]
            hidden_in = jnp.dot(in_rows, weight_up, preferred_element_type=jnp.float32)
            activated = jax.nn.silu(hidden_in).astype(jnp.bfloat16)
            expert_out = jnp.dot(activated, weight_down, preferred_element_type=jnp.float32).astype(jnp.bfloat16)
            act_grad = jnp.dot(dy_rows, weight_down.T, preferred_element_type=jnp.float32)
            pre_grad = (act_grad * silu_grad(hidden_in)).astype(jnp.bfloat16)
            row_grad = jnp.dot(pre_grad, weight_up.T, preferred_element_type=jnp.float32).astype(jnp.bfloat16)
            part_up = jnp.dot(in_rows.T, pre_grad, preferred_element_type=jnp.float32).astype(jnp.bfloat16)
            part_down = jnp.dot(activated.T, dy_rows, preferred_element_type=jnp.float32).astype(jnp.bfloat16)
            target = jnp.where(filled, pair_index, pair_total).astype(jnp.int32)
            return (expert_out, row_grad, target, part_up, part_down)
        outs_all, grads_all, targets, parts_up, parts_down = lax.map(per_expert, expert_range)
        flat_targets = targets.reshape(-1)
        pair_out = jnp.zeros((pair_total, D), jnp.bfloat16).at[flat_targets].set(outs_all.reshape(-1, D), mode='drop')
        pair_grad = jnp.zeros((pair_total, D), jnp.bfloat16).at[flat_targets].set(grads_all.reshape(-1, D), mode='drop')
        weighted = group_gates.reshape(group_tokens, TOP, 1) * pair_out.reshape(group_tokens, TOP, D).astype(jnp.float32)
        layer_part = lax.optimization_barrier(jnp.sum(weighted, axis=1)).astype(jnp.bfloat16)
        grad_part = lax.optimization_barrier(jnp.sum(pair_grad.reshape(group_tokens, TOP, D).astype(jnp.float32), axis=1)).astype(jnp.bfloat16)
        new_carry = (sum_up + parts_up.astype(jnp.float32), sum_down + parts_down.astype(jnp.float32))
        return (new_carry, (layer_part, grad_part))
    start = (jnp.zeros((EXPERTS, D, H), jnp.float32), jnp.zeros((EXPERTS, H, D), jnp.float32))
    totals, pieces = lax.scan(group_step, start, (tokens_group, cot_group, ids_group, gates_group))
    sum_up, sum_down = totals
    layer_parts, grad_parts = pieces
    inverse = jnp.argsort(expert_home).astype(jnp.int32)
    slot_up = sum_up[inverse].astype(jnp.bfloat16)
    slot_down = sum_down[inverse].astype(jnp.bfloat16)
    grad_up = jnp.concatenate([slot_up, slot_up], axis=0)
    grad_down = jnp.concatenate([slot_down, slot_down], axis=0)
    return (layer_parts.reshape(-1, D), grad_parts.reshape(-1, D), grad_up, grad_down)
```

```python
import functools

import jax
import jax.numpy as jnp
from jax import lax
from jax.experimental import pallas as pl
from jax.experimental.pallas import tpu as pltpu
from jax.sharding import PartitionSpec as P

MESH = pl.DeviceIdType.MESH
NX = 4
LANES = 128
f32, bf16, i32 = jnp.float32, jnp.bfloat16, jnp.int32


def place():
    dp, ex = lax.axis_index("dp"), lax.axis_index("expert")
    return dp, ex // NX, ex % NX


def z_shift(o, core, w):
    return o - w * ((o + core) // (w // 2 + 1))


def contract(a, b, da, db):
    return lax.dot_general(a, b, (((da,), (db,)), ((), ())), preferred_element_type=f32)


def spread(rows, stage, out_ref, which):
    count, width = rows.shape
    chunks = width // LANES
    for c in range(chunks):
        stage[pl.ds(c, count, stride=chunks), :] = rows[:, c * LANES : (c + 1) * LANES]
    out_ref[which] = stage[...].astype(bf16)


def gather_rows(in_ref, which, stage, chunks):
    stage[...] = in_ref[which].astype(f32)
    count = stage.shape[0] // chunks
    return jnp.concatenate(
        [stage[pl.ds(c, count, stride=chunks), :] for c in range(chunks)], axis=1
    )


def prep_kernel(nz, cap, ids_ref, gates_ref, home_ref, tok_ref, cot_ref, send_ref, sel_ref, stage):
    _, z, x = place()
    w = nz // 2
    tok_count = ids_ref.shape[0]
    experts = home_ref.shape[1]
    rows = experts * cap
    home = home_ref[...]
    shift = NX.bit_length() - 1
    block_z = ((home >> shift) + (nz - z)) & (w - 1)
    block_x = ((home & (NX - 1)) + (NX - x)) & (NX - 1)
    first_row = (block_z * NX + block_x).astype(f32) * float(cap)

    ids = ids_ref[...]
    which = lax.broadcasted_iota(i32, (tok_count, experts), 1)
    earlier = lax.broadcasted_iota(i32, (tok_count, tok_count), 0) > lax.broadcasted_iota(
        i32, (tok_count, tok_count), 1
    )
    earlier = earlier.astype(f32).astype(bf16)
    row_no = lax.broadcasted_iota(i32, (tok_count, rows), 1)
    base = first_row
    sels = []
    for k in range(2):
        hot = (ids[:, k : k + 1] == which).astype(f32)
        before = contract(earlier, hot.astype(bf16), 1, 0)
        row = jnp.sum(hot * (base + before), axis=1, keepdims=True).astype(i32)
        sels.append((row == row_no).astype(f32).astype(bf16))
        base = base + jnp.sum(hot, axis=0, keepdims=True)
    sel_ref[0] = sels[0]
    sel_ref[1] = sels[1]
    spread(contract(sels[0] + sels[1], tok_ref[...], 0, 0), stage, send_ref, 0)
    cot = cot_ref[...].astype(f32)
    scaled = [(gates_ref[:, k : k + 1] * cot).astype(bf16) for k in range(2)]
    picked = contract(sels[0], scaled[0], 0, 0) + contract(sels[1], scaled[1], 0, 0)
    spread(picked, stage, send_ref, 1)


def far_order(i, w):
    k = i // NX
    o = w // 2 + k // 2 - (k % 2) * (2 * (k // 2) + 1)
    return o, NX - 1 - i % NX


def block_refs(src, dst, b, size):
    at = pl.ds(pl.multiple_of(b * size, size), size)
    return src.at[:, at, :], dst.at[:, at, :]


def exchange_blocks(nz, sign, src, dst, send_sem, recv_sem):
    dp, z, x = place()
    core, w = dp % 2, nz // 2
    blocks = w * NX
    size = src.shape[1] // blocks

    def copy(i):
        o, xo = far_order(i, w)
        b = o * NX + xo
        to_z = (z + nz + sign * z_shift(o, core, w)) % nz
        to_x = (x + NX + sign * xo) % NX
        s, d = block_refs(src, dst, b, size)
        return pltpu.make_async_remote_copy(
            src_ref=s,
            dst_ref=d,
            send_sem=send_sem.at[b],
            recv_sem=recv_sem.at[b],
            device_id=(dp, to_z * NX + to_x),
            device_id_type=MESH,
        )

    return copy, blocks - 1


def greet_blocks(nz, sign, barrier):
    dp, z, x = place()
    core, w = dp % 2, nz // 2

    def tell(i, _):
        o, xo = far_order(i, w)
        to_z = (z + nz - sign * z_shift(o, core, w)) % nz
        to_x = (x + NX - sign * xo) % NX
        pl.semaphore_signal(
            barrier, inc=1, device_id=(dp, to_z * NX + to_x), device_id_type=MESH
        )
        return 0

    lax.fori_loop(0, w * NX - 1, tell, 0)
    return w * NX - 1


def each(count, act):
    def step(i, _):
        act(i)
        return 0

    lax.fori_loop(0, count, step, 0)


def dispatch_kernel(nz, send_ref, recv_ref, send_sem, recv_sem, own_sem):
    barrier = pltpu.get_barrier_semaphore()
    size = send_ref.shape[1] // (nz // 2 * NX)
    own = pltpu.make_async_copy(*block_refs(send_ref, recv_ref, 0, size), own_sem)
    own.start()
    pl.semaphore_wait(barrier, greet_blocks(nz, 1, barrier))
    copy, count = exchange_blocks(nz, 1, send_ref, recv_ref, send_sem, recv_sem)
    each(count, lambda i: copy(i).start())
    own.wait()
    each(count, lambda i: copy(i).wait())


def expert_kernel(recv_ref, up_ref, down_ref, ret_ref, gup_ref, gdn_ref, stage):
    up, down = up_ref[...], down_ref[...]
    chunks = up.shape[0] // LANES
    in_f = gather_rows(recv_ref, 0, stage, chunks)
    in_rows = in_f.astype(bf16)
    dy = gather_rows(recv_ref, 1, stage, chunks).astype(bf16)
    pre = contract(in_rows, up, 1, 0)
    sig = 1.0 / (1.0 + jnp.exp(-pre))
    act = (pre * sig).astype(bf16)
    spread(contract(act, down, 1, 0), stage, ret_ref, 0)
    act_grad = contract(dy, down, 1, 1)
    pre_grad = (act_grad * (sig * (1.0 + pre * (1.0 - sig)))).astype(bf16)
    spread(contract(pre_grad, up, 1, 1), stage, ret_ref, 1)
    shards, depth, _ = gup_ref.shape
    for j in range(shards):
        part = in_rows[:, j * depth : (j + 1) * depth]
        gup_ref[j] = contract(part, pre_grad, 0, 0).astype(bf16)
    act_t = act.astype(f32).T.astype(bf16)
    for j in range(0, shards, 2):
        both = contract(act_t, dy[:, j * depth : (j + 2) * depth], 1, 0).astype(bf16)
        gdn_ref[j] = both[:, :depth]
        gdn_ref[j + 1] = both[:, depth:]


def give_back_kernel(
    nz, ret_ref, gup_ref, gdn_ref, back_ref, fup_ref, fdn_ref,
    core_up, core_dn, sum_up, sum_dn, pair_up, pair_dn, mine_up, mine_dn,
    one_up, one_dn, tot_up, tot_dn, far_up, far_dn,
    send_sem, recv_sem, own_sem, s_sem, r_sem,
):
    dp, z, x = place()
    core, y = dp % 2, dp // 2
    ex = z * NX + x
    barrier = pltpu.get_barrier_semaphore()
    size = ret_ref.shape[1] // (nz // 2 * NX)
    partner = (y * 2 + 1 - core, ex)
    flip1, flip3 = y + 1 - 2 * (y % 2), 3 - y
    beside1 = (flip1 * 2 + core, ex)
    beside3 = (flip3 * 2 + core, ex)
    across = (dp, ((z + nz // 2) % nz) * NX + x)

    own = pltpu.make_async_copy(*block_refs(ret_ref, back_ref, 0, size), own_sem)
    own.start()
    for other in (partner, beside1, beside3, across):
        pl.semaphore_signal(barrier, inc=1, device_id=other, device_id_type=MESH)
    pl.semaphore_wait(barrier, 4 + greet_blocks(nz, -1, barrier))

    def remote(n, src, dst, to):
        return pltpu.make_async_remote_copy(
            src_ref=src, dst_ref=dst, send_sem=s_sem.at[n], recv_sem=r_sem.at[n],
            device_id=to, device_id_type=MESH,
        )

    swap_up = remote(0, gup_ref.at[:, 1 - core], core_up, partner)
    swap_dn = remote(1, gdn_ref.at[:, 1 - core], core_dn, partner)
    swap_up.start()
    swap_dn.start()
    copy, count = exchange_blocks(nz, -1, ret_ref, back_ref, send_sem, recv_sem)
    each(count, lambda i: copy(i).start())

    def add(a, b):
        return (a.astype(f32) + b.astype(f32)).astype(bf16)

    first = []
    for n, swap, part, rx, sums, got, near, near_far, far, to in (
        (2, swap_up, gup_ref, core_up, sum_up, pair_up, flip1, 3 - flip1, flip3, beside1),
        (3, swap_dn, gdn_ref, core_dn, sum_dn, pair_dn, flip3, 3 - flip1, flip1, beside3),
    ):
        swap.wait()
        sums[0] = add(part[near, core], rx[near])
        sums[1] = add(part[near_far, core], rx[near_far])
        step = remote(n, sums.at[0:2], got, to)
        step.start()
        sums[2] = add(part[y, core], rx[y])
        sums[3] = add(part[far, core], rx[far])
        first.append(step)
    second = []
    for n, step, sums, got, mine, one, to in (
        (4, first[0], sum_up, pair_up, mine_up, one_up, beside3),
        (5, first[1], sum_dn, pair_dn, mine_dn, one_dn, beside1),
    ):
        step.wait()
        mine[0] = add(sums[3], got[1])
        step = remote(n, mine.at[0], one, to)
        step.start()
        mine[1] = add(sums[2], got[0])
        second.append(step)
    last = []
    for n, step, mine, one, tot, got in (
        (6, second[0], mine_up, one_up, tot_up, far_up),
        (7, second[1], mine_dn, one_dn, tot_dn, far_dn),
    ):
        step.wait()
        tot[...] = add(mine[1], one[...])
        step = remote(n, tot, got, across)
        step.start()
        last.append(step)
    own.wait()
    each(count, lambda i: copy(i).wait())
    for step, tot, got, out in (
        (last[0], tot_up, far_up, fup_ref),
        (last[1], tot_dn, far_dn, fdn_ref),
    ):
        step.wait()
        out[...] = add(tot[...], got[...])


def combine_kernel(back_ref, sel_ref, gates_ref, out_ref, grad_ref, stage):
    chunks = out_ref.shape[1] // LANES
    outs = gather_rows(back_ref, 0, stage, chunks).astype(bf16)
    first, second = sel_ref[0], sel_ref[1]
    total = gates_ref[:, 0:1] * contract(first, outs, 1, 0)
    total = total + gates_ref[:, 1:2] * contract(second, outs, 1, 0)
    out_ref[...] = total.astype(bf16)
    grads = gather_rows(back_ref, 1, stage, chunks).astype(bf16)
    grad_ref[...] = contract(first + second, grads, 1, 0).astype(bf16)


def shape(*dims, dtype=bf16):
    return jax.ShapeDtypeStruct(dims, dtype)


VM = pl.BlockSpec(memory_space=pltpu.VMEM)


def local(nz, ndp, tokens, cotangent, expert_ids, gates, expert_home, up_weight, down_weight):
    tok_count, width = tokens.shape
    hidden = up_weight.shape[2]
    experts = expert_home.shape[0]
    cap = 5 * tok_count * 2 // (4 * experts)
    rows = experts * cap
    chunks = width // LANES
    flat = rows * chunks
    blocks = experts
    depth = width // ndp
    ny = ndp // 2
    stage = pltpu.VMEM((flat, LANES), f32)
    dma = pltpu.SemaphoreType.DMA

    send, sel = pl.pallas_call(
        functools.partial(prep_kernel, nz, cap),
        out_shape=(shape(2, flat, LANES), shape(2, tok_count, rows)),
        in_specs=[VM] * 5,
        out_specs=(VM, VM),
        scratch_shapes=[stage],
        name="prep",
    )(expert_ids, gates, expert_home.reshape(1, experts), tokens, cotangent)

    recv = pl.pallas_call(
        functools.partial(dispatch_kernel, nz),
        out_shape=shape(2, flat, LANES),
        in_specs=[VM],
        out_specs=VM,
        scratch_shapes=[dma((blocks,)), dma((blocks,)), dma],
        compiler_params=pltpu.CompilerParams(collective_id=0, has_side_effects=True),
        name="dispatch",
    )(send)

    ret, gup, gdn = pl.pallas_call(
        expert_kernel,
        out_shape=(shape(2, flat, LANES), shape(ndp, depth, hidden), shape(ndp, hidden, depth)),
        in_specs=[VM] * 3,
        out_specs=(VM,) * 3,
        scratch_shapes=[stage],
        name="experts",
    )(recv, up_weight.reshape(width, hidden), down_weight.reshape(hidden, width))

    def both(*lead):
        return [pltpu.VMEM(lead + (depth, hidden), bf16), pltpu.VMEM(lead + (hidden, depth), bf16)]

    back, fup, fdn = pl.pallas_call(
        functools.partial(give_back_kernel, nz),
        out_shape=(shape(2, flat, LANES), shape(depth, hidden), shape(hidden, depth)),
        in_specs=[VM] * 3,
        out_specs=(VM,) * 3,
        scratch_shapes=both(ny) + both(ny) + both(2) + both(2) + both() + both() + both()
        + [dma((blocks,)), dma((blocks,)), dma, dma((8,)), dma((8,))],
        compiler_params=pltpu.CompilerParams(collective_id=1, has_side_effects=True),
        name="give_back",
    )(ret, gup.reshape(ny, 2, depth, hidden), gdn.reshape(ny, 2, hidden, depth))

    layer_out, grad_tokens = pl.pallas_call(
        combine_kernel,
        out_shape=(shape(tok_count, width), shape(tok_count, width)),
        in_specs=[VM] * 3,
        out_specs=(VM, VM),
        scratch_shapes=[stage],
        name="combine",
    )(back, sel, gates)
    return layer_out, grad_tokens, fup[None], fdn[None]


def solution(mesh):
    rows = P(("dp", "expert"), None)
    held = P("expert", None, None)
    return jax.shard_map(
        functools.partial(local, mesh.shape["expert"] // NX, mesh.shape["dp"]),
        mesh=mesh,
        in_specs=(rows, rows, rows, rows, P(), held, held),
        out_specs=(rows, rows, P("expert", "dp", None), P("expert", None, "dp")),
        check_vma=False,
    )
```

```python
import functools

import jax
import jax.numpy as jnp
from jax import lax
from jax.experimental import pallas as pl
from jax.experimental.pallas import tpu as pltpu
from jax.sharding import PartitionSpec as P

MESH = pl.DeviceIdType.MESH
NX = 4
LANES = 128
f32, bf16, i32 = jnp.float32, jnp.bfloat16, jnp.int32


def place():
    dp, ex = lax.axis_index("dp"), lax.axis_index("expert")
    return dp, ex // NX, ex % NX


def z_shift(o, core, w):
    return o - w * ((o + core) // (w // 2 + 1))


def contract(a, b, da, db):
    return lax.dot_general(a, b, (((da,), (db,)), ((), ())), preferred_element_type=f32)


def spread(rows, stage, out_ref):
    count, width = rows.shape
    chunks = width // LANES
    for c in range(chunks):
        stage[pl.ds(c, count, stride=chunks), :] = rows[:, c * LANES : (c + 1) * LANES]
    out_ref[...] = stage[...].astype(bf16)


def gather_rows(flat, stage, chunks):
    stage[...] = flat.astype(f32)
    count = stage.shape[0] // chunks
    parts = [stage[pl.ds(c, count, stride=chunks), :] for c in range(chunks)]
    return jnp.concatenate(parts, axis=1).astype(bf16)


def iota(shape, dim):
    return lax.broadcasted_iota(i32, shape, dim)


def as_column(row):
    n = row.shape[1]
    eye = iota((n, n), 0) == iota((n, n), 1)
    return jnp.sum(jnp.where(eye, row, 0.0), axis=1, keepdims=True)


def selections(nz, cap, ids, home):
    _, z, x = place()
    w = nz // 2
    tok_count, experts = ids.shape[1], home.shape[1]
    rows = experts * cap
    slot = as_column(home.astype(f32)).astype(i32)
    shift = NX.bit_length() - 1
    block_z = ((slot >> shift) + (nz - z)) & (w - 1)
    block_x = ((slot & (NX - 1)) + (NX - x)) & (NX - 1)
    base = (block_z * NX + block_x).astype(f32) * float(cap)
    earlier = iota((tok_count, tok_count), 0) < iota((tok_count, tok_count), 1)
    earlier = earlier.astype(f32).astype(bf16)
    row_no = iota((rows, tok_count), 0)
    sels = []
    for k in range(2):
        hot = (iota((experts, tok_count), 0) == ids[k : k + 1, :]).astype(f32)
        before = contract(hot.astype(bf16), earlier, 1, 0)
        row = jnp.sum(hot * (base + before), axis=0, keepdims=True).astype(i32)
        sels.append((row_no == row).astype(f32).astype(bf16))
        base = base + jnp.sum(hot, axis=1, keepdims=True)
    return sels


def far_order(i, w):
    k = i // NX
    o = w // 2 + k // 2 - (k % 2) * (2 * (k // 2) + 1)
    return o, NX - 1 - i % NX


def peer(nz, sign, i):
    dp, z, x = place()
    w = nz // 2
    o, xo = far_order(i, w)
    to_z = (z + nz + sign * z_shift(o, dp % 2, w)) % nz
    to_x = (x + NX + sign * xo) % NX
    return o * NX + xo, (dp, to_z * NX + to_x)


def each(count, act):
    def step(i, _):
        act(i)
        return 0

    lax.fori_loop(0, count, step, 0)


def add(a, b):
    return (a.astype(f32) + b.astype(f32)).astype(bf16)


def layer_kernel(
    nz, cap, subs,
    ids_ref, gates_ref, home_ref, tok_hbm, cot_hbm, up_hbm, down_hbm,
    back_ref, sel_ref, tot_up, tot_dn, far_up, far_dn,
    tok_ref, cot_ref, up_ref, down_ref, stage, send_x, send_y, recv_x, recv_y, ret_x, ret_y,
    part_up, part_dn, core_up, core_dn, sum_up, sum_dn, pair_up, pair_dn,
    mine_up, mine_dn, one_up, one_dn, ring_up, ring_dn,
    in_sem, block_send, block_recv, s_sem, r_sem, ring_send, ring_recv,
):
    dp, z, x = place()
    core, y = dp % 2, dp // 2
    ex = z * NX + x
    blocks = nz // 2 * NX
    others = blocks - 1
    size = send_x.shape[0] // blocks
    partner = (y * 2 + 1 - core, ex)
    flip1, flip3 = y + 1 - 2 * (y % 2), 3 - y
    beside1 = (flip1 * 2 + core, ex)
    beside3 = (flip3 * 2 + core, ex)

    barrier = pltpu.get_barrier_semaphore()

    def tell(to):
        pl.semaphore_signal(barrier, inc=1, device_id=to, device_id_type=MESH)

    def tell_both(i):
        tell(peer(nz, 1, i)[1])
        tell(peer(nz, -1, i)[1])

    each(others, tell_both)
    for to in (partner, beside1, beside3):
        tell(to)
    loads = [
        pltpu.make_async_copy(src, dst, in_sem.at[n])
        for n, (src, dst) in enumerate(
            ((tok_hbm, tok_ref), (cot_hbm, cot_ref), (up_hbm, up_ref), (down_hbm, down_ref))
        )
    ]
    for load in loads:
        load.start()

    def block_copy(n, sign, src, dst):
        def copy(i):
            b, to = peer(nz, sign, i)
            at = pl.ds(pl.multiple_of(b * size, size), size)
            return pltpu.make_async_remote_copy(
                src_ref=src.at[at, :], dst_ref=dst.at[at, :],
                send_sem=block_send.at[n, b], recv_sem=block_recv.at[n, b],
                device_id=to, device_id_type=MESH,
            )

        return copy

    give_x = block_copy(0, 1, send_x, recv_x)
    give_y = block_copy(1, 1, send_y, recv_y)
    return_x = block_copy(2, -1, ret_x, back_ref.at[0])
    return_y = block_copy(3, -1, ret_y, back_ref.at[1])

    def remote(n, src, dst, to):
        return pltpu.make_async_remote_copy(
            src_ref=src, dst_ref=dst, send_sem=s_sem.at[n], recv_sem=r_sem.at[n],
            device_id=to, device_id_type=MESH,
        )

    first, second = selections(nz, cap, ids_ref[...], home_ref[...])
    sel_ref[0] = first
    sel_ref[1] = second
    loads[0].wait()
    spread(contract(first + second, tok_ref[...], 1, 0), stage, send_x)
    pl.semaphore_wait(barrier, 2 * others + 3)
    each(others, lambda i: give_x(i).start())
    recv_x[0:size, :] = send_x[0:size, :]
    loads[1].wait()
    cot = cot_ref[...].astype(f32)
    picked = contract(first, (as_column(gates_ref[0:1, :]) * cot).astype(bf16), 1, 0)
    picked += contract(second, (as_column(gates_ref[1:2, :]) * cot).astype(bf16), 1, 0)
    spread(picked, stage, send_y)
    each(others, lambda i: give_y(i).start())
    recv_y[0:size, :] = send_y[0:size, :]

    loads[2].wait()
    loads[3].wait()
    chunks = up_ref.shape[0] // LANES
    each(others, lambda i: give_x(i).wait_recv())
    in_rows = gather_rows(recv_x[...], stage, chunks)
    pre = contract(in_rows, up_ref[...], 1, 0)
    sig = 1.0 / (1.0 + jnp.exp(-pre))
    act_wide = pre * sig
    slope = sig * (1.0 + pre * (1.0 - sig))
    spread(contract(act_wide.astype(bf16), down_ref[...], 1, 0), stage, ret_x)
    act_t = act_wide.T.astype(bf16)
    back_ref[0, 0:size, :] = ret_x[0:size, :]

    each(others, lambda i: give_y(i).wait_recv())
    each(others, lambda i: return_x(i).start())
    dy = gather_rows(recv_y[...], stage, chunks)
    pre_grad = (contract(dy, down_ref[...], 1, 1) * slope).astype(bf16)
    ny, _, depth, _ = part_up.shape
    for j in range(2 * ny):
        cut = in_rows[:, j * depth : (j + 1) * depth]
        part_up[j // 2, j % 2] = contract(cut, pre_grad, 0, 0).astype(bf16)
    swap_up = remote(0, part_up.at[:, 1 - core], core_up, partner)
    swap_up.start()
    for j in range(ny):
        two = contract(act_t, dy[:, 2 * j * depth : (2 * j + 2) * depth], 1, 0).astype(bf16)
        part_dn[j, 0] = two[:, :depth]
        part_dn[j, 1] = two[:, depth:]
    swap_dn = remote(1, part_dn.at[:, 1 - core], core_dn, partner)
    swap_dn.start()
    spread(contract(pre_grad, up_ref[...], 1, 1), stage, ret_y)
    each(others, lambda i: return_y(i).start())
    back_ref[1, 0:size, :] = ret_y[0:size, :]

    steps = []
    for n, swap, part, rx, sums, got, near, near_far, far, to in (
        (2, swap_up, part_up, core_up, sum_up, pair_up, flip1, 3 - flip1, flip3, beside1),
        (3, swap_dn, part_dn, core_dn, sum_dn, pair_dn, flip3, 3 - flip1, flip1, beside3),
    ):
        swap.wait()
        sums[0] = add(part[near, core], rx[near])
        sums[1] = add(part[near_far, core], rx[near_far])
        step = remote(n, sums.at[0:2], got, to)
        step.start()
        sums[2] = add(part[y, core], rx[y])
        sums[3] = add(part[far, core], rx[far])
        steps.append(step)
    later = []
    for n, step, sums, got, mine, one, to in (
        (4, steps[0], sum_up, pair_up, mine_up, one_up, beside3),
        (5, steps[1], sum_dn, pair_dn, mine_dn, one_dn, beside1),
    ):
        step.wait()
        mine[0] = add(sums[3], got[1])
        step = remote(n, mine.at[0], one, to)
        step.start()
        mine[1] = add(sums[2], got[0])
        later.append(step)

    half = nz // 2

    def hop(d, j, src, k):
        total, ring = ((tot_up, ring_up), (tot_dn, ring_dn))[d]
        rows = total.shape[0] // subs
        at = pl.ds(j * rows, rows)
        to_z = (z + (1, nz - 1)[d]) % nz
        return pltpu.make_async_remote_copy(
            src_ref=total.at[at] if src is None else ring.at[src, at],
            dst_ref=ring.at[k, at],
            send_sem=ring_send.at[d, k, j], recv_sem=ring_recv.at[d, k, j],
            device_id=(dp, to_z * NX + x), device_id_type=MESH,
        )

    for d, (step, mine, one, tot) in enumerate(
        ((later[0], mine_up, one_up, tot_up), (later[1], mine_dn, one_dn, tot_dn))
    ):
        step.wait()
        tot[...] = add(mine[1], one[...])
        for j in range(subs):
            hop(d, j, None, 0).start()
    both = [(d, j) for j in range(subs) for d in range(2)]

    def forward(k):
        for d, j in both:
            hop(d, j, k, k).wait_recv()
            hop(d, j, k, k + 1).start()

    each(half - 1, forward)
    for d, j in both:
        hop(d, j, half - 1, half - 1).wait_recv()
    far_up[...] = ring_up[half - 1]
    far_dn[...] = ring_dn[half - 1]

    def drain(k):
        for d, j in both:
            hop(d, j, k, k).wait_send()

    each(half, drain)
    for give in (give_x, give_y):
        each(others, lambda i: give(i).wait_send())
    for give in (return_x, return_y):
        each(others, lambda i: give(i).wait())


def combine_kernel(
    back_ref, sel_ref, gates_ref, tot_up, tot_dn, far_up, far_dn,
    out_ref, grad_ref, fup_ref, fdn_ref, stage,
):
    chunks = out_ref.shape[1] // LANES
    outs = gather_rows(back_ref[0], stage, chunks)
    first, second = sel_ref[0], sel_ref[1]
    total = as_column(gates_ref[0:1, :]) * contract(first, outs, 0, 0)
    total += as_column(gates_ref[1:2, :]) * contract(second, outs, 0, 0)
    out_ref[...] = total.astype(bf16)
    grads = gather_rows(back_ref[1], stage, chunks)
    grad_ref[...] = contract(first + second, grads, 0, 0).astype(bf16)
    fup_ref[...] = add(tot_up[...], far_up[...])
    fdn_ref[...] = add(tot_dn[...], far_dn[...])


def shape(*dims, dtype=bf16):
    return jax.ShapeDtypeStruct(dims, dtype)


VM = pl.BlockSpec(memory_space=pltpu.VMEM)
HBM = pl.BlockSpec(memory_space=pl.ANY)
SUBS = 4


def local(nz, ndp, tokens, cotangent, expert_ids, gates, expert_home, up_weight, down_weight):
    tok_count, width = tokens.shape
    hidden = up_weight.shape[2]
    experts = expert_home.shape[0]
    cap = 5 * tok_count * 2 // (4 * experts)
    rows = experts * cap
    flat = rows * (width // LANES)
    depth = width // ndp
    ny = ndp // 2
    half = nz // 2
    stage = pltpu.VMEM((flat, LANES), f32)
    dma = pltpu.SemaphoreType.DMA
    up_shape, dn_shape = (depth, hidden), (hidden, depth)

    def both(*lead):
        return [pltpu.VMEM(lead + up_shape, bf16), pltpu.VMEM(lead + dn_shape, bf16)]

    gates_t = gates.T
    back, sel, *totals = pl.pallas_call(
        functools.partial(layer_kernel, nz, cap, SUBS),
        out_shape=(shape(2, flat, LANES), shape(2, rows, tok_count))
        + (shape(*up_shape), shape(*dn_shape)) * 2,
        in_specs=[VM] * 3 + [HBM] * 4,
        out_specs=(VM,) * 6,
        scratch_shapes=[
            pltpu.VMEM((tok_count, width), bf16),
            pltpu.VMEM((tok_count, width), bf16),
            pltpu.VMEM((width, hidden), bf16),
            pltpu.VMEM((hidden, width), bf16),
            stage,
        ]
        + [pltpu.VMEM((flat, LANES), bf16)] * 6
        + both(ny, 2) + both(ny) + both(ny) + both(2) + both(2) + both() + both(half)
        + [
            dma((4,)), dma((4, experts)), dma((4, experts)), dma((6,)), dma((6,)),
            dma((2, half, SUBS)), dma((2, half, SUBS)),
        ],
        compiler_params=pltpu.CompilerParams(collective_id=0, has_side_effects=True),
        name="layer",
    )(
        expert_ids.T, gates_t, expert_home.reshape(1, experts), tokens, cotangent,
        up_weight.reshape(width, hidden), down_weight.reshape(hidden, width),
    )

    layer_out, grad_tokens, fup, fdn = pl.pallas_call(
        combine_kernel,
        out_shape=(shape(tok_count, width),) * 2 + (shape(*up_shape), shape(*dn_shape)),
        in_specs=[VM] * 7,
        out_specs=(VM,) * 4,
        scratch_shapes=[stage],
        name="combine",
    )(back, sel, gates_t, *totals)
    return layer_out, grad_tokens, fup[None], fdn[None]


def solution(mesh):
    rows = P(("dp", "expert"), None)
    held = P("expert", None, None)
    return jax.shard_map(
        functools.partial(local, mesh.shape["expert"] // NX, mesh.shape["dp"]),
        mesh=mesh,
        in_specs=(rows, rows, rows, rows, P(), held, held),
        out_specs=(rows, rows, P("expert", "dp", None), P("expert", None, "dp")),
        check_vma=False,
    )
```

```python
import functools

import jax
import jax.numpy as jnp
from jax import lax
from jax.experimental import pallas as pl
from jax.experimental.pallas import tpu as pltpu
from jax.sharding import PartitionSpec as P

MESH = pl.DeviceIdType.MESH
NX = 4
LANES = 128
f32, bf16, i32 = jnp.float32, jnp.bfloat16, jnp.int32


def place():
    dp, ex = lax.axis_index("dp"), lax.axis_index("expert")
    return dp, ex // NX, ex % NX


def z_shift(o, core, w):
    return o - w * ((o + core) // (w // 2 + 1))


def contract(a, b, da, db):
    return lax.dot_general(a, b, (((da,), (db,)), ((), ())), preferred_element_type=f32)


def spread(rows, stage, out_ref):
    count, width = rows.shape
    chunks = width // LANES
    for c in range(chunks):
        stage[pl.ds(c, count, stride=chunks), :] = rows[:, c * LANES : (c + 1) * LANES]
    out_ref[...] = stage[...].astype(bf16)


def gather_rows(flat, stage, chunks):
    stage[...] = flat.astype(f32)
    count = stage.shape[0] // chunks
    parts = [stage[pl.ds(c, count, stride=chunks), :] for c in range(chunks)]
    return jnp.concatenate(parts, axis=1).astype(bf16)


def iota(shape, dim):
    return lax.broadcasted_iota(i32, shape, dim)


def as_column(row):
    n = row.shape[1]
    eye = iota((n, n), 0) == iota((n, n), 1)
    return jnp.sum(jnp.where(eye, row, 0.0), axis=1, keepdims=True)


def selections(nz, cap, ids, home):
    _, z, x = place()
    w = nz // 2
    tok_count, experts = ids.shape[1], home.shape[1]
    rows = experts * cap
    slot = as_column(home.astype(f32)).astype(i32)
    shift = NX.bit_length() - 1
    block_z = ((slot >> shift) + (nz - z)) & (w - 1)
    block_x = ((slot & (NX - 1)) + (NX - x)) & (NX - 1)
    base = (block_z * NX + block_x).astype(f32) * float(cap)
    earlier = iota((tok_count, tok_count), 0) < iota((tok_count, tok_count), 1)
    earlier = earlier.astype(f32).astype(bf16)
    row_no = iota((rows, tok_count), 0)
    sels = []
    for k in range(2):
        hot = (iota((experts, tok_count), 0) == ids[k : k + 1, :]).astype(f32)
        before = contract(hot.astype(bf16), earlier, 1, 0)
        row = jnp.sum(hot * (base + before), axis=0, keepdims=True).astype(i32)
        sels.append((row_no == row).astype(f32).astype(bf16))
        base = base + jnp.sum(hot, axis=1, keepdims=True)
    return sels


def far_order(i, w):
    k = i // NX
    o = w // 2 + k // 2 - (k % 2) * (2 * (k // 2) + 1)
    return o, NX - 1 - i % NX


def peer(nz, sign, i):
    dp, z, x = place()
    w = nz // 2
    o, xo = far_order(i, w)
    to_z = (z + nz + sign * z_shift(o, dp % 2, w)) % nz
    to_x = (x + NX + sign * xo) % NX
    return o * NX + xo, (dp, to_z * NX + to_x)


def each(count, act, start=0):
    def step(i, _):
        act(i)
        return 0

    lax.fori_loop(start, count, step, 0)


def add(a, b):
    return (a.astype(f32) + b.astype(f32)).astype(bf16)


def layer_kernel(
    nz, cap, subs, early,
    ids_ref, gates_ref, home_ref, tok_hbm, cot_hbm, up_hbm, down_hbm,
    out_ref, grad_ref, fup_ref, fdn_ref,
    tok_ref, cot_ref, up_ref, down_ref, stage, send_x, send_y, recv_x, recv_y, ret_x, ret_y,
    back_x, back_y, tot_up, tot_dn,
    part_up, part_dn, core_up, core_dn, sum_up, sum_dn, pair_up, pair_dn,
    mine_up, mine_dn, one_up, one_dn, ring_up, ring_dn,
    in_sem, block_send, block_recv, s_sem, r_sem, ring_send, ring_recv,
):
    dp, z, x = place()
    core, y = dp % 2, dp // 2
    ex = z * NX + x
    blocks = nz // 2 * NX
    others = blocks - 1
    size = send_x.shape[0] // blocks
    partner = (y * 2 + 1 - core, ex)
    flip1, flip3 = y + 1 - 2 * (y % 2), 3 - y
    beside1 = (flip1 * 2 + core, ex)
    beside3 = (flip3 * 2 + core, ex)

    barrier = pltpu.get_barrier_semaphore()

    def tell(to):
        pl.semaphore_signal(barrier, inc=1, device_id=to, device_id_type=MESH)

    def tell_both(i):
        tell(peer(nz, 1, i)[1])
        tell(peer(nz, -1, i)[1])

    each(others, tell_both)
    for to in (partner, beside1, beside3):
        tell(to)
    loads = [
        pltpu.make_async_copy(src, dst, in_sem.at[n])
        for n, (src, dst) in enumerate(
            ((tok_hbm, tok_ref), (cot_hbm, cot_ref), (up_hbm, up_ref), (down_hbm, down_ref))
        )
    ]
    for load in loads:
        load.start()

    def block_copy(n, sign, src, dst):
        def copy(i):
            b, to = peer(nz, sign, i)
            at = pl.ds(pl.multiple_of(b * size, size), size)
            return pltpu.make_async_remote_copy(
                src_ref=src.at[at, :], dst_ref=dst.at[at, :],
                send_sem=block_send.at[n, b], recv_sem=block_recv.at[n, b],
                device_id=to, device_id_type=MESH,
            )

        return copy

    give_x = block_copy(0, 1, send_x, recv_x)
    give_y = block_copy(1, 1, send_y, recv_y)
    return_x = block_copy(2, -1, ret_x, back_x)
    return_y = block_copy(3, -1, ret_y, back_y)

    def remote(n, src, dst, to):
        return pltpu.make_async_remote_copy(
            src_ref=src, dst_ref=dst, send_sem=s_sem.at[n], recv_sem=r_sem.at[n],
            device_id=to, device_id_type=MESH,
        )

    first, second = selections(nz, cap, ids_ref[...], home_ref[...])
    loads[0].wait()
    spread(contract(first + second, tok_ref[...], 1, 0), stage, send_x)
    pl.semaphore_wait(barrier, 2 * others + 3)
    each(others, lambda i: give_x(i).start())
    recv_x[0:size, :] = send_x[0:size, :]
    loads[1].wait()
    cot = cot_ref[...].astype(f32)
    picked = contract(first, (as_column(gates_ref[0:1, :]) * cot).astype(bf16), 1, 0)
    picked += contract(second, (as_column(gates_ref[1:2, :]) * cot).astype(bf16), 1, 0)
    spread(picked, stage, send_y)
    each(others, lambda i: give_y(i).start())
    recv_y[0:size, :] = send_y[0:size, :]

    loads[2].wait()
    loads[3].wait()
    chunks = up_ref.shape[0] // LANES
    each(others, lambda i: give_x(i).wait_recv())
    in_rows = gather_rows(recv_x[...], stage, chunks)
    pre = contract(in_rows, up_ref[...], 1, 0)
    sig = 1.0 / (1.0 + jnp.exp(-pre))
    act_wide = pre * sig
    slope = sig * (1.0 + pre * (1.0 - sig))
    spread(contract(act_wide.astype(bf16), down_ref[...], 1, 0), stage, ret_x)
    act_t = act_wide.T.astype(bf16)
    back_x[0:size, :] = ret_x[0:size, :]
    each(early, lambda i: return_x(i).start())

    each(others, lambda i: give_y(i).wait_recv())
    each(others, lambda i: return_x(i).start(), early)
    dy = gather_rows(recv_y[...], stage, chunks)
    pre_grad = (contract(dy, down_ref[...], 1, 1) * slope).astype(bf16)
    ny, _, depth, _ = part_up.shape
    for j in range(2 * ny):
        cut = in_rows[:, j * depth : (j + 1) * depth]
        part_up[j // 2, j % 2] = contract(cut, pre_grad, 0, 0).astype(bf16)
    swap_up = remote(0, part_up.at[:, 1 - core], core_up, partner)
    swap_up.start()
    for j in range(ny):
        two = contract(act_t, dy[:, 2 * j * depth : (2 * j + 2) * depth], 1, 0).astype(bf16)
        part_dn[j, 0] = two[:, :depth]
        part_dn[j, 1] = two[:, depth:]
    swap_dn = remote(1, part_dn.at[:, 1 - core], core_dn, partner)
    swap_dn.start()
    spread(contract(pre_grad, up_ref[...], 1, 1), stage, ret_y)
    each(others, lambda i: return_y(i).start())
    back_y[0:size, :] = ret_y[0:size, :]

    steps = []
    for n, swap, part, rx, sums, got, near, near_far, far, to in (
        (2, swap_up, part_up, core_up, sum_up, pair_up, flip1, 3 - flip1, flip3, beside1),
        (3, swap_dn, part_dn, core_dn, sum_dn, pair_dn, flip3, 3 - flip1, flip1, beside3),
    ):
        swap.wait()
        sums[1] = add(part[near_far, core], rx[near_far])
        pair = [remote(n, sums.at[1], got.at[1], to), remote(n + 4, sums.at[0], got.at[0], to)]
        pair[0].start()
        sums[0] = add(part[near, core], rx[near])
        pair[1].start()
        sums[3] = add(part[far, core], rx[far])
        sums[2] = add(part[y, core], rx[y])
        steps.append(pair)
    later = []
    for n, pair, sums, got, mine, one, to in (
        (4, steps[0], sum_up, pair_up, mine_up, one_up, beside3),
        (5, steps[1], sum_dn, pair_dn, mine_dn, one_dn, beside1),
    ):
        pair[0].wait()
        mine[0] = add(sums[3], got[1])
        step = remote(n, mine.at[0], one, to)
        step.start()
        later.append(step)
    for pair, sums, got, mine in (
        (steps[0], sum_up, pair_up, mine_up),
        (steps[1], sum_dn, pair_dn, mine_dn),
    ):
        pair[1].wait()
        mine[1] = add(sums[2], got[0])

    half = nz // 2

    def hop(d, j, src, k):
        total, ring = ((tot_up, ring_up), (tot_dn, ring_dn))[d]
        rows = total.shape[0] // subs
        at = pl.ds(j * rows, rows)
        to_z = (z + (1, nz - 1)[d]) % nz
        return pltpu.make_async_remote_copy(
            src_ref=total.at[at] if src is None else ring.at[src, at],
            dst_ref=ring.at[k, at],
            send_sem=ring_send.at[d, k, j], recv_sem=ring_recv.at[d, k, j],
            device_id=(dp, to_z * NX + x), device_id_type=MESH,
        )

    for d, (step, mine, one, tot) in enumerate(
        ((later[0], mine_up, one_up, tot_up), (later[1], mine_dn, one_dn, tot_dn))
    ):
        step.wait()
        tot[...] = add(mine[1], one[...])
        for j in range(subs):
            hop(d, j, None, 0).start()
    both = [(d, j) for j in range(subs) for d in range(2)]

    def forward(k):
        for d, j in both:
            hop(d, j, k, k).wait_recv()
            hop(d, j, k, k + 1).start()

    each(half - 1, forward)
    each(others, lambda i: return_x(i).wait_recv())
    outs = gather_rows(back_x[...], stage, chunks)
    total = as_column(gates_ref[0:1, :]) * contract(first, outs, 0, 0)
    total += as_column(gates_ref[1:2, :]) * contract(second, outs, 0, 0)
    out_ref[...] = total.astype(bf16)
    each(others, lambda i: return_y(i).wait_recv())
    grads = gather_rows(back_y[...], stage, chunks)
    grad_ref[...] = contract(first + second, grads, 0, 0).astype(bf16)
    for d, j in both:
        hop(d, j, half - 1, half - 1).wait_recv()
    fup_ref[...] = add(tot_up[...], ring_up[half - 1])
    fdn_ref[...] = add(tot_dn[...], ring_dn[half - 1])

    def drain(k):
        for d, j in both:
            hop(d, j, k, k).wait_send()

    each(half, drain)
    for moved in (give_x, give_y, return_x, return_y):
        each(others, lambda i: moved(i).wait_send())


def hand_on_kernel(*refs):
    *arrays, sem = refs
    half = len(arrays) // 2
    copies = [
        pltpu.make_async_copy(arrays[n], arrays[half + n], sem.at[n]) for n in range(half)
    ]
    for copy in copies:
        copy.start()
    for copy in copies:
        copy.wait()


def shape(*dims, dtype=bf16):
    return jax.ShapeDtypeStruct(dims, dtype)


VM = pl.BlockSpec(memory_space=pltpu.VMEM)
HBM = pl.BlockSpec(memory_space=pltpu.HBM)
SUBS = 4
LAYER_VMEM, HAND_VMEM = 54150 * 1024, 2**20
EARLY = 10


def local(nz, ndp, tokens, cotangent, expert_ids, gates, expert_home, up_weight, down_weight):
    tok_count, width = tokens.shape
    hidden = up_weight.shape[2]
    experts = expert_home.shape[0]
    cap = 5 * tok_count * 2 // (4 * experts)
    rows = experts * cap
    flat = rows * (width // LANES)
    depth = width // ndp
    ny = ndp // 2
    half = nz // 2
    stage = pltpu.VMEM((flat, LANES), f32)
    dma = pltpu.SemaphoreType.DMA
    up_shape, dn_shape = (depth, hidden), (hidden, depth)

    def both(*lead):
        return [pltpu.VMEM(lead + up_shape, bf16), pltpu.VMEM(lead + dn_shape, bf16)]

    results = (shape(tok_count, width),) * 2 + (shape(*up_shape), shape(*dn_shape))
    early = min(EARLY, experts - 1)
    made = pl.pallas_call(
        functools.partial(layer_kernel, nz, cap, SUBS, early),
        out_shape=results,
        in_specs=[VM] * 3 + [HBM] * 4,
        out_specs=(VM,) * 4,
        scratch_shapes=[
            pltpu.VMEM((tok_count, width), bf16),
            pltpu.VMEM((tok_count, width), bf16),
            pltpu.VMEM((width, hidden), bf16),
            pltpu.VMEM((hidden, width), bf16),
            stage,
        ]
        + [pltpu.VMEM((flat, LANES), bf16)] * 8
        + both() + both(ny, 2) + both(ny) + both(ny) + both(2) + both(2) + both() + both(half)
        + [
            dma((4,)), dma((4, experts)), dma((4, experts)), dma((8,)), dma((8,)),
            dma((2, half, SUBS)), dma((2, half, SUBS)),
        ],
        compiler_params=pltpu.CompilerParams(
            collective_id=0, has_side_effects=True, vmem_limit_bytes=LAYER_VMEM
        ),
        name="layer",
    )(
        expert_ids.T, gates.T, expert_home.reshape(1, experts), tokens, cotangent,
        up_weight.reshape(width, hidden), down_weight.reshape(hidden, width),
    )
    layer_out, grad_tokens, fup, fdn = pl.pallas_call(
        hand_on_kernel,
        out_shape=results,
        in_specs=[VM] * 4,
        out_specs=(HBM,) * 4,
        scratch_shapes=[dma((4,))],
        compiler_params=pltpu.CompilerParams(vmem_limit_bytes=HAND_VMEM),
        name="hand_on",
    )(*made)
    return layer_out, grad_tokens, fup[None], fdn[None]


def solution(mesh):
    rows = P(("dp", "expert"), None)
    held = P("expert", None, None)
    return jax.shard_map(
        functools.partial(local, mesh.shape["expert"] // NX, mesh.shape["dp"]),
        mesh=mesh,
        in_specs=(rows, rows, rows, rows, P(), held, held),
        out_specs=(rows, rows, P("expert", "dp", None), P("expert", None, "dp")),
        check_vma=False,
    )
```

```python
import functools

import jax
import jax.numpy as jnp
from jax import lax
from jax.experimental import pallas as pl
from jax.experimental.pallas import tpu as pltpu
from jax.sharding import PartitionSpec as P

MESH = pl.DeviceIdType.MESH
NX = 4
LANES = 128
f32, bf16, i32 = jnp.float32, jnp.bfloat16, jnp.int32


def place():
    dp, ex = lax.axis_index("dp"), lax.axis_index("expert")
    return dp, ex // NX, ex % NX


def z_shift(o, core, w):
    return o - w * ((o + core) // (w // 2 + 1))


def contract(a, b, da, db):
    return lax.dot_general(a, b, (((da,), (db,)), ((), ())), preferred_element_type=f32)


def spread(rows, stage, out_ref):
    count, width = rows.shape
    chunks = width // LANES
    for c in range(chunks):
        stage[pl.ds(c, count, stride=chunks), :] = rows[:, c * LANES : (c + 1) * LANES]
    out_ref[...] = stage[...].astype(bf16)


def gather_rows(flat, stage, chunks):
    stage[...] = flat.astype(f32)
    count = stage.shape[0] // chunks
    parts = [stage[pl.ds(c, count, stride=chunks), :] for c in range(chunks)]
    return jnp.concatenate(parts, axis=1).astype(bf16)


def iota(shape, dim):
    return lax.broadcasted_iota(i32, shape, dim)


def as_column(row):
    n = row.shape[1]
    eye = iota((n, n), 0) == iota((n, n), 1)
    return jnp.sum(jnp.where(eye, row, 0.0), axis=1, keepdims=True)


def selections(nz, cap, ids, home):
    _, z, x = place()
    w = nz // 2
    tok_count, experts = ids.shape[1], home.shape[1]
    rows = experts * cap
    slot = as_column(home.astype(f32)).astype(i32)
    shift = NX.bit_length() - 1
    block_z = ((slot >> shift) + (nz - z)) & (w - 1)
    block_x = ((slot & (NX - 1)) + (NX - x)) & (NX - 1)
    base = (block_z * NX + block_x).astype(f32) * float(cap)
    earlier = iota((tok_count, tok_count), 0) < iota((tok_count, tok_count), 1)
    earlier = earlier.astype(f32).astype(bf16)
    row_no = iota((rows, tok_count), 0)
    sels = []
    for k in range(2):
        hot = (iota((experts, tok_count), 0) == ids[k : k + 1, :]).astype(f32)
        before = contract(hot.astype(bf16), earlier, 1, 0)
        row = jnp.sum(hot * (base + before), axis=0, keepdims=True).astype(i32)
        sels.append((row_no == row).astype(f32).astype(bf16))
        base = base + jnp.sum(hot, axis=1, keepdims=True)
    return sels


def far_order(i, w):
    k = i // NX
    o = w // 2 + k // 2 - (k % 2) * (2 * (k // 2) + 1)
    return o, NX - 1 - i % NX


def peer(nz, sign, i):
    dp, z, x = place()
    w = nz // 2
    o, xo = far_order(i, w)
    to_z = (z + nz + sign * z_shift(o, dp % 2, w)) % nz
    to_x = (x + NX + sign * xo) % NX
    return o * NX + xo, (dp, to_z * NX + to_x)


def each(count, act, start=0):
    def step(i, _):
        act(i)
        return 0

    lax.fori_loop(start, count, step, 0)


def add(a, b):
    return (a.astype(f32) + b.astype(f32)).astype(bf16)


def layer_kernel(
    nz, cap, subs, early,
    ids_hbm, gates_hbm, home_hbm, tok_hbm, cot_hbm, up_hbm, down_hbm,
    out_ref, grad_ref, fup_ref, fdn_ref,
    ids_ref, gates_ref, home_ref, tok_ref, cot_ref, up_ref, down_ref, stage, send_x, send_y, recv_x, recv_y, ret_x, ret_y,
    back_x, back_y, tot_up, tot_dn,
    part_up, part_dn, core_up, core_dn, sum_up, sum_dn, pair_up, pair_dn,
    mine_up, mine_dn, one_up, one_dn, ring_up, ring_dn,
    in_sem, block_send, block_recv, s_sem, r_sem, ring_send, ring_recv,
):
    dp, z, x = place()
    core, y = dp % 2, dp // 2
    ex = z * NX + x
    blocks = nz // 2 * NX
    others = blocks - 1
    size = send_x.shape[0] // blocks
    partner = (y * 2 + 1 - core, ex)
    flip1, flip3 = y + 1 - 2 * (y % 2), 3 - y
    beside1 = (flip1 * 2 + core, ex)
    beside3 = (flip3 * 2 + core, ex)

    barrier = pltpu.get_barrier_semaphore()

    def tell(to):
        pl.semaphore_signal(barrier, inc=1, device_id=to, device_id_type=MESH)

    def tell_both(i):
        tell(peer(nz, 1, i)[1])
        tell(peer(nz, -1, i)[1])

    loads = [
        pltpu.make_async_copy(src, dst, in_sem.at[n])
        for n, (src, dst) in enumerate(
            (
                (tok_hbm, tok_ref), (cot_hbm, cot_ref), (up_hbm, up_ref), (down_hbm, down_ref),
                (ids_hbm, ids_ref), (gates_hbm, gates_ref), (home_hbm, home_ref),
            )
        )
    ]
    for n in (4, 6, 0, 5, 1, 2, 3):
        loads[n].start()
    each(others, tell_both)
    for to in (partner, beside1, beside3):
        tell(to)

    def block_copy(n, sign, src, dst):
        def copy(i):
            b, to = peer(nz, sign, i)
            at = pl.ds(pl.multiple_of(b * size, size), size)
            return pltpu.make_async_remote_copy(
                src_ref=src.at[at, :], dst_ref=dst.at[at, :],
                send_sem=block_send.at[n, b], recv_sem=block_recv.at[n, b],
                device_id=to, device_id_type=MESH,
            )

        return copy

    give_x = block_copy(0, 1, send_x, recv_x)
    give_y = block_copy(1, 1, send_y, recv_y)
    return_x = block_copy(2, -1, ret_x, back_x)
    return_y = block_copy(3, -1, ret_y, back_y)

    def remote(n, src, dst, to):
        return pltpu.make_async_remote_copy(
            src_ref=src, dst_ref=dst, send_sem=s_sem.at[n], recv_sem=r_sem.at[n],
            device_id=to, device_id_type=MESH,
        )

    loads[4].wait()
    loads[6].wait()
    first, second = selections(nz, cap, ids_ref[...], home_ref[...])
    loads[0].wait()
    spread(contract(first + second, tok_ref[...], 1, 0), stage, send_x)
    pl.semaphore_wait(barrier, 2 * others + 3)
    each(others, lambda i: give_x(i).start())
    recv_x[0:size, :] = send_x[0:size, :]
    loads[5].wait()
    loads[1].wait()
    cot = cot_ref[...].astype(f32)
    picked = contract(first, (as_column(gates_ref[0:1, :]) * cot).astype(bf16), 1, 0)
    picked += contract(second, (as_column(gates_ref[1:2, :]) * cot).astype(bf16), 1, 0)
    spread(picked, stage, send_y)
    each(others, lambda i: give_y(i).start())
    recv_y[0:size, :] = send_y[0:size, :]

    loads[2].wait()
    loads[3].wait()
    chunks = up_ref.shape[0] // LANES
    each(others, lambda i: give_x(i).wait_recv())
    in_rows = gather_rows(recv_x[...], stage, chunks)
    pre = contract(in_rows, up_ref[...], 1, 0)
    sig = 1.0 / (1.0 + jnp.exp(-pre))
    act_wide = pre * sig
    slope = sig * (1.0 + pre * (1.0 - sig))
    spread(contract(act_wide.astype(bf16), down_ref[...], 1, 0), stage, ret_x)
    act_t = act_wide.T.astype(bf16)
    back_x[0:size, :] = ret_x[0:size, :]
    each(early, lambda i: return_x(i).start())

    each(others, lambda i: give_y(i).wait_recv())
    each(others, lambda i: return_x(i).start(), early)
    dy = gather_rows(recv_y[...], stage, chunks)
    pre_grad = (contract(dy, down_ref[...], 1, 1) * slope).astype(bf16)
    ny, _, depth, _ = part_up.shape
    for j in range(2 * ny):
        cut = in_rows[:, j * depth : (j + 1) * depth]
        part_up[j // 2, j % 2] = contract(cut, pre_grad, 0, 0).astype(bf16)
    swap_up = remote(0, part_up.at[:, 1 - core], core_up, partner)
    swap_up.start()
    for j in range(ny):
        two = contract(act_t, dy[:, 2 * j * depth : (2 * j + 2) * depth], 1, 0).astype(bf16)
        part_dn[j, 0] = two[:, :depth]
        part_dn[j, 1] = two[:, depth:]
    swap_dn = remote(1, part_dn.at[:, 1 - core], core_dn, partner)
    swap_dn.start()
    spread(contract(pre_grad, up_ref[...], 1, 1), stage, ret_y)
    each(others, lambda i: return_y(i).start())
    back_y[0:size, :] = ret_y[0:size, :]

    steps = []
    for n, swap, part, rx, sums, got, near, near_far, far, to in (
        (2, swap_up, part_up, core_up, sum_up, pair_up, flip1, 3 - flip1, flip3, beside1),
        (3, swap_dn, part_dn, core_dn, sum_dn, pair_dn, flip3, 3 - flip1, flip1, beside3),
    ):
        swap.wait()
        sums[1] = add(part[near_far, core], rx[near_far])
        pair = [remote(n, sums.at[1], got.at[1], to), remote(n + 4, sums.at[0], got.at[0], to)]
        pair[0].start()
        sums[0] = add(part[near, core], rx[near])
        pair[1].start()
        sums[3] = add(part[far, core], rx[far])
        sums[2] = add(part[y, core], rx[y])
        steps.append(pair)
    later = []
    for n, pair, sums, got, mine, one, to in (
        (4, steps[0], sum_up, pair_up, mine_up, one_up, beside3),
        (5, steps[1], sum_dn, pair_dn, mine_dn, one_dn, beside1),
    ):
        pair[0].wait()
        mine[0] = add(sums[3], got[1])
        step = remote(n, mine.at[0], one, to)
        step.start()
        later.append(step)
    for pair, sums, got, mine in (
        (steps[0], sum_up, pair_up, mine_up),
        (steps[1], sum_dn, pair_dn, mine_dn),
    ):
        pair[1].wait()
        mine[1] = add(sums[2], got[0])

    half = nz // 2

    def hop(d, j, src, k):
        total, ring = ((tot_up, ring_up), (tot_dn, ring_dn))[d]
        rows = total.shape[0] // subs
        at = pl.ds(j * rows, rows)
        to_z = (z + (1, nz - 1)[d]) % nz
        return pltpu.make_async_remote_copy(
            src_ref=total.at[at] if src is None else ring.at[src, at],
            dst_ref=ring.at[k, at],
            send_sem=ring_send.at[d, k, j], recv_sem=ring_recv.at[d, k, j],
            device_id=(dp, to_z * NX + x), device_id_type=MESH,
        )

    for d, (step, mine, one, tot) in enumerate(
        ((later[0], mine_up, one_up, tot_up), (later[1], mine_dn, one_dn, tot_dn))
    ):
        step.wait()
        tot[...] = add(mine[1], one[...])
        for j in range(subs):
            hop(d, j, None, 0).start()
    both = [(d, j) for j in range(subs) for d in range(2)]

    def forward(k):
        for d, j in both:
            hop(d, j, k, k).wait_recv()
            hop(d, j, k, k + 1).start()

    each(half - 1, forward)
    each(others, lambda i: return_x(i).wait_recv())
    outs = gather_rows(back_x[...], stage, chunks)
    total = as_column(gates_ref[0:1, :]) * contract(first, outs, 0, 0)
    total += as_column(gates_ref[1:2, :]) * contract(second, outs, 0, 0)
    out_ref[...] = total.astype(bf16)
    each(others, lambda i: return_y(i).wait_recv())
    grads = gather_rows(back_y[...], stage, chunks)
    grad_ref[...] = contract(first + second, grads, 0, 0).astype(bf16)
    for d, j in both:
        hop(d, j, half - 1, half - 1).wait_recv()
    fup_ref[...] = add(tot_up[...], ring_up[half - 1])
    fdn_ref[...] = add(tot_dn[...], ring_dn[half - 1])

    def drain(k):
        for d, j in both:
            hop(d, j, k, k).wait_send()

    each(half, drain)
    for moved in (give_x, give_y, return_x, return_y):
        each(others, lambda i: moved(i).wait_send())


def hand_on_kernel(*refs):
    *arrays, sem = refs
    half = len(arrays) // 2
    copies = [
        pltpu.make_async_copy(arrays[n], arrays[half + n], sem.at[n]) for n in range(half)
    ]
    for copy in copies:
        copy.start()
    for copy in copies:
        copy.wait()


def shape(*dims, dtype=bf16):
    return jax.ShapeDtypeStruct(dims, dtype)


VM = pl.BlockSpec(memory_space=pltpu.VMEM)
HBM = pl.BlockSpec(memory_space=pltpu.HBM)
SUBS = 4
LAYER_VMEM, HAND_VMEM = 48 * 2**20, 2**20
EARLY = 10


def local(nz, ndp, tokens, cotangent, expert_ids, gates, expert_home, up_weight, down_weight):
    tok_count, width = tokens.shape
    hidden = up_weight.shape[2]
    experts = expert_home.shape[0]
    cap = 5 * tok_count * 2 // (4 * experts)
    rows = experts * cap
    flat = rows * (width // LANES)
    depth = width // ndp
    ny = ndp // 2
    half = nz // 2
    stage = pltpu.VMEM((flat, LANES), f32)
    dma = pltpu.SemaphoreType.DMA
    up_shape, dn_shape = (depth, hidden), (hidden, depth)

    def both(*lead):
        return [pltpu.VMEM(lead + up_shape, bf16), pltpu.VMEM(lead + dn_shape, bf16)]

    results = (shape(tok_count, width),) * 2 + (shape(*up_shape), shape(*dn_shape))
    early = min(EARLY, experts - 1)
    made = pl.pallas_call(
        functools.partial(layer_kernel, nz, cap, SUBS, early),
        out_shape=results,
        in_specs=[HBM] * 7,
        out_specs=(VM,) * 4,
        scratch_shapes=[
            pltpu.VMEM((2, tok_count), i32),
            pltpu.VMEM((2, tok_count), f32),
            pltpu.VMEM((1, experts), i32),
            pltpu.VMEM((tok_count, width), bf16),
            pltpu.VMEM((tok_count, width), bf16),
            pltpu.VMEM((width, hidden), bf16),
            pltpu.VMEM((hidden, width), bf16),
            stage,
        ]
        + [pltpu.VMEM((flat, LANES), bf16)] * 8
        + both() + both(ny, 2) + both(ny) + both(ny) + both(2) + both(2) + both() + both(half)
        + [
            dma((7,)), dma((4, experts)), dma((4, experts)), dma((8,)), dma((8,)),
            dma((2, half, SUBS)), dma((2, half, SUBS)),
        ],
        compiler_params=pltpu.CompilerParams(
            collective_id=0, has_side_effects=True, vmem_limit_bytes=LAYER_VMEM
        ),
        name="layer",
    )(
        *(
            pltpu.with_memory_space_constraint(array, pltpu.HBM)
            for array in (
                expert_ids.T, gates.T, expert_home.reshape(1, experts), tokens, cotangent,
                up_weight.reshape(width, hidden), down_weight.reshape(hidden, width),
            )
        )
    )
    layer_out, grad_tokens, fup, fdn = pl.pallas_call(
        hand_on_kernel,
        out_shape=results,
        in_specs=[VM] * 4,
        out_specs=(HBM,) * 4,
        scratch_shapes=[dma((4,))],
        compiler_params=pltpu.CompilerParams(vmem_limit_bytes=HAND_VMEM),
        name="hand_on",
    )(*made)
    return layer_out, grad_tokens, fup[None], fdn[None]


def solution(mesh):
    rows = P(("dp", "expert"), None)
    held = P("expert", None, None)
    return jax.shard_map(
        functools.partial(local, mesh.shape["expert"] // NX, mesh.shape["dp"]),
        mesh=mesh,
        in_specs=(rows, rows, rows, rows, P(), held, held),
        out_specs=(rows, rows, P("expert", "dp", None), P("expert", None, "dp")),
        check_vma=False,
    )
```

```python
import functools

import jax
import jax.numpy as jnp
from jax import lax
from jax.experimental import pallas as pl
from jax.experimental.pallas import tpu as pltpu
from jax.sharding import PartitionSpec as P

MESH = pl.DeviceIdType.MESH
NX = 4
LANES = 128
f32, bf16, i32 = jnp.float32, jnp.bfloat16, jnp.int32


def place():
    dp, ex = lax.axis_index("dp"), lax.axis_index("expert")
    return dp, ex // NX, ex % NX


def z_shift(o, core, w):
    return o - w * lax.div(o + core + (w // 2 - 1), w)


def contract(a, b, da, db):
    return lax.dot_general(a, b, (((da,), (db,)), ((), ())), preferred_element_type=f32)


def spread(rows, stage, out_ref):
    count, width = rows.shape
    chunks = width // LANES
    for c in range(chunks):
        stage[pl.ds(c, count, stride=chunks), :] = rows[:, c * LANES : (c + 1) * LANES]
    out_ref[...] = stage[...].astype(bf16)


def gather_rows(flat, stage, chunks):
    stage[...] = flat.astype(f32)
    count = stage.shape[0] // chunks
    parts = [stage[pl.ds(c, count, stride=chunks), :] for c in range(chunks)]
    return jnp.concatenate(parts, axis=1).astype(bf16)


def iota(shape, dim):
    return lax.broadcasted_iota(i32, shape, dim)


def as_column(row):
    n = row.shape[1]
    eye = iota((n, n), 0) == iota((n, n), 1)
    return jnp.sum(jnp.where(eye, row, 0.0), axis=1, keepdims=True)


def selections(nz, cap, ids, home):
    _, z, x = place()
    w = nz // 2
    tok_count, experts = ids.shape[1], home.shape[1]
    rows = experts * cap
    slot = as_column(home.astype(f32)).astype(i32)
    shift = NX.bit_length() - 1
    block_z = ((slot >> shift) + (nz - z)) & (w - 1)
    block_x = ((slot & (NX - 1)) + (NX - x)) & (NX - 1)
    base = (block_z * NX + block_x).astype(f32) * float(cap)
    earlier = iota((tok_count, tok_count), 0) < iota((tok_count, tok_count), 1)
    earlier = earlier.astype(f32).astype(bf16)
    row_no = iota((rows, tok_count), 0)
    sels = []
    for k in range(2):
        hot = (iota((experts, tok_count), 0) == ids[k : k + 1, :]).astype(f32)
        before = contract(hot.astype(bf16), earlier, 1, 0)
        row = jnp.sum(hot * (base + before), axis=0, keepdims=True).astype(i32)
        sels.append((row_no == row).astype(f32).astype(bf16))
        base = base + jnp.sum(hot, axis=1, keepdims=True)
    return sels


def far_order(i, w):
    k = lax.div(i, NX)
    twos = lax.div(k, 2)
    o = w // 2 + twos - lax.rem(k, 2) * (2 * twos + 1)
    return o, NX - 1 - lax.rem(i, NX)


def peer(nz, sign, i):
    dp, z, x = place()
    w = nz // 2
    o, xo = far_order(i, w)
    to_z = lax.rem(z + nz + sign * z_shift(o, dp % 2, w), nz)
    to_x = lax.rem(x + NX + sign * xo, NX)
    return o * NX + xo, (dp, to_z * NX + to_x)


def each(count, act, start=0):
    def step(i, _):
        act(i)
        return 0

    lax.fori_loop(start, count, step, 0)


def add(a, b):
    return (a.astype(f32) + b.astype(f32)).astype(bf16)


def layer_kernel(
    nz, cap, subs, early,
    ids_hbm, gates_hbm, home_hbm, tok_hbm, cot_hbm, up_hbm, down_hbm,
    out_ref, grad_ref, fup_ref, fdn_ref,
    ids_ref, gates_ref, home_ref, tok_ref, cot_ref, up_ref, down_ref, stage, send_x, send_y, recv_x, recv_y, ret_x, ret_y,
    back_x, back_y, tot_up, tot_dn,
    part_up, part_dn, core_up, core_dn, sum_up, sum_dn, pair_up, pair_dn,
    mine_up, mine_dn, one_up, one_dn, ring_up, ring_dn,
    in_sem, block_send, block_recv, s_sem, r_sem, ring_send, ring_recv,
):
    dp, z, x = place()
    core, y = dp % 2, dp // 2
    ex = z * NX + x
    blocks = nz // 2 * NX
    others = blocks - 1
    size = send_x.shape[0] // blocks
    partner = (y * 2 + 1 - core, ex)
    flip1, flip3 = y + 1 - 2 * (y % 2), 3 - y
    beside1 = (flip1 * 2 + core, ex)
    beside3 = (flip3 * 2 + core, ex)

    barrier = pltpu.get_barrier_semaphore()

    def tell(to):
        pl.semaphore_signal(barrier, inc=1, device_id=to, device_id_type=MESH)

    def tell_both(i):
        tell(peer(nz, 1, i)[1])
        tell(peer(nz, -1, i)[1])

    loads = [
        pltpu.make_async_copy(src, dst, in_sem.at[n])
        for n, (src, dst) in enumerate(
            (
                (tok_hbm, tok_ref), (cot_hbm, cot_ref), (up_hbm, up_ref), (down_hbm, down_ref),
                (ids_hbm, ids_ref), (gates_hbm, gates_ref), (home_hbm, home_ref),
            )
        )
    ]
    for n in (4, 6, 0, 5, 1, 2, 3):
        loads[n].start()
    each(others, tell_both)
    for to in (partner, beside1, beside3):
        tell(to)

    def block_copy(n, sign, src, dst):
        def copy(i):
            b, to = peer(nz, sign, i)
            at = pl.ds(pl.multiple_of(b * size, size), size)
            return pltpu.make_async_remote_copy(
                src_ref=src.at[at, :], dst_ref=dst.at[at, :],
                send_sem=block_send.at[n], recv_sem=block_recv.at[n],
                device_id=to, device_id_type=MESH,
            )

        return copy

    def all_blocks(n, src, dst):
        rest = pl.ds(size, others * size)
        return pltpu.make_async_remote_copy(
            src_ref=src.at[rest, :], dst_ref=dst.at[rest, :],
            send_sem=block_send.at[n], recv_sem=block_recv.at[n],
            device_id=partner, device_id_type=MESH,
        )

    whole = [
        all_blocks(n, src, dst)
        for n, (src, dst) in enumerate(
            ((send_x, recv_x), (send_y, recv_y), (ret_x, back_x), (ret_y, back_y))
        )
    ]

    give_x = block_copy(0, 1, send_x, recv_x)
    give_y = block_copy(1, 1, send_y, recv_y)
    return_x = block_copy(2, -1, ret_x, back_x)
    return_y = block_copy(3, -1, ret_y, back_y)

    def remote(n, src, dst, to):
        return pltpu.make_async_remote_copy(
            src_ref=src, dst_ref=dst, send_sem=s_sem.at[n], recv_sem=r_sem.at[n],
            device_id=to, device_id_type=MESH,
        )

    loads[4].wait()
    loads[6].wait()
    first, second = selections(nz, cap, ids_ref[...], home_ref[...])
    loads[0].wait()
    spread(contract(first + second, tok_ref[...], 1, 0), stage, send_x)
    pl.semaphore_wait(barrier, 2 * others + 3)
    each(others, lambda i: give_x(i).start())
    recv_x[0:size, :] = send_x[0:size, :]
    loads[5].wait()
    loads[1].wait()
    cot = cot_ref[...].astype(f32)
    picked = contract(first, (as_column(gates_ref[0:1, :]) * cot).astype(bf16), 1, 0)
    picked += contract(second, (as_column(gates_ref[1:2, :]) * cot).astype(bf16), 1, 0)
    spread(picked, stage, send_y)
    each(others, lambda i: give_y(i).start())
    recv_y[0:size, :] = send_y[0:size, :]

    loads[2].wait()
    loads[3].wait()
    chunks = up_ref.shape[0] // LANES
    whole[0].wait_recv()
    in_rows = gather_rows(recv_x[...], stage, chunks)
    pre = contract(in_rows, up_ref[...], 1, 0)
    sig = 1.0 / (1.0 + jnp.exp(-pre))
    act_wide = pre * sig
    slope = sig * (1.0 + pre * (1.0 - sig))
    spread(contract(act_wide.astype(bf16), down_ref[...], 1, 0), stage, ret_x)
    act_t = act_wide.T.astype(bf16)
    back_x[0:size, :] = ret_x[0:size, :]
    each(early, lambda i: return_x(i).start())

    whole[1].wait_recv()
    each(others, lambda i: return_x(i).start(), early)
    dy = gather_rows(recv_y[...], stage, chunks)
    pre_grad = (contract(dy, down_ref[...], 1, 1) * slope).astype(bf16)
    ny, _, depth, _ = part_up.shape
    for j in range(2 * ny):
        cut = in_rows[:, j * depth : (j + 1) * depth]
        part_up[j // 2, j % 2] = contract(cut, pre_grad, 0, 0).astype(bf16)
    swap_up = remote(0, part_up.at[:, 1 - core], core_up, partner)
    swap_up.start()
    for j in range(ny):
        two = contract(act_t, dy[:, 2 * j * depth : (2 * j + 2) * depth], 1, 0).astype(bf16)
        part_dn[j, 0] = two[:, :depth]
        part_dn[j, 1] = two[:, depth:]
    swap_dn = remote(1, part_dn.at[:, 1 - core], core_dn, partner)
    swap_dn.start()
    spread(contract(pre_grad, up_ref[...], 1, 1), stage, ret_y)
    each(others, lambda i: return_y(i).start())
    back_y[0:size, :] = ret_y[0:size, :]

    steps = []
    for n, swap, part, rx, sums, got, near, near_far, far, to in (
        (2, swap_up, part_up, core_up, sum_up, pair_up, flip1, 3 - flip1, flip3, beside1),
        (3, swap_dn, part_dn, core_dn, sum_dn, pair_dn, flip3, 3 - flip1, flip1, beside3),
    ):
        swap.wait()
        sums[1] = add(part[near_far, core], rx[near_far])
        pair = [remote(n, sums.at[1], got.at[1], to), remote(n + 4, sums.at[0], got.at[0], to)]
        pair[0].start()
        sums[0] = add(part[near, core], rx[near])
        pair[1].start()
        sums[3] = add(part[far, core], rx[far])
        sums[2] = add(part[y, core], rx[y])
        steps.append(pair)
    later = []
    for n, pair, sums, got, mine, one, to in (
        (4, steps[0], sum_up, pair_up, mine_up, one_up, beside3),
        (5, steps[1], sum_dn, pair_dn, mine_dn, one_dn, beside1),
    ):
        pair[0].wait()
        mine[0] = add(sums[3], got[1])
        step = remote(n, mine.at[0], one, to)
        step.start()
        later.append(step)
    for pair, sums, got, mine in (
        (steps[0], sum_up, pair_up, mine_up),
        (steps[1], sum_dn, pair_dn, mine_dn),
    ):
        pair[1].wait()
        mine[1] = add(sums[2], got[0])

    half = nz // 2

    def hop(d, j, src, k):
        total, ring = ((tot_up, ring_up), (tot_dn, ring_dn))[d]
        rows = total.shape[0] // subs
        at = pl.ds(j * rows, rows)
        to_z = (z + (1, nz - 1)[d]) % nz
        return pltpu.make_async_remote_copy(
            src_ref=total.at[at] if src is None else ring.at[src, at],
            dst_ref=ring.at[k, at],
            send_sem=ring_send.at[d, k, j], recv_sem=ring_recv.at[d, k, j],
            device_id=(dp, to_z * NX + x), device_id_type=MESH,
        )

    for d, (step, mine, one, tot) in enumerate(
        ((later[0], mine_up, one_up, tot_up), (later[1], mine_dn, one_dn, tot_dn))
    ):
        step.wait()
        tot[...] = add(mine[1], one[...])
        for j in range(subs):
            hop(d, j, None, 0).start()
    both = [(d, j) for j in range(subs) for d in range(2)]

    def forward(k):
        for d, j in both:
            hop(d, j, k, k).wait_recv()
            hop(d, j, k, k + 1).start()

    each(half - 1, forward)
    whole[2].wait_recv()
    outs = gather_rows(back_x[...], stage, chunks)
    total = as_column(gates_ref[0:1, :]) * contract(first, outs, 0, 0)
    total += as_column(gates_ref[1:2, :]) * contract(second, outs, 0, 0)
    out_ref[...] = total.astype(bf16)
    whole[3].wait_recv()
    grads = gather_rows(back_y[...], stage, chunks)
    grad_ref[...] = contract(first + second, grads, 0, 0).astype(bf16)

    def drain(k):
        for d, j in both:
            hop(d, j, k, k).wait_send()

    for exchange in whole:
        exchange.wait_send()
    each(half - 1, drain)
    for d, j in both:
        hop(d, j, half - 1, half - 1).wait_recv()
    fup_ref[...] = add(tot_up[...], ring_up[half - 1])
    fdn_ref[...] = add(tot_dn[...], ring_dn[half - 1])
    drain(half - 1)


def hand_on_kernel(*refs):
    *arrays, sem = refs
    half = len(arrays) // 2
    copies = [
        pltpu.make_async_copy(arrays[n], arrays[half + n], sem.at[n]) for n in range(half)
    ]
    for copy in copies:
        copy.start()
    for copy in copies:
        copy.wait()


def shape(*dims, dtype=bf16):
    return jax.ShapeDtypeStruct(dims, dtype)


VM = pl.BlockSpec(memory_space=pltpu.VMEM)
HBM = pl.BlockSpec(memory_space=pltpu.HBM)
SUBS = 4
LAYER_VMEM, HAND_VMEM = 48 * 2**20, 2**20
EARLY = 10


def local(nz, ndp, tokens, cotangent, expert_ids, gates, expert_home, up_weight, down_weight):
    tok_count, width = tokens.shape
    hidden = up_weight.shape[2]
    experts = expert_home.shape[0]
    cap = 5 * tok_count * 2 // (4 * experts)
    rows = experts * cap
    flat = rows * (width // LANES)
    depth = width // ndp
    ny = ndp // 2
    half = nz // 2
    stage = pltpu.VMEM((flat, LANES), f32)
    dma = pltpu.SemaphoreType.DMA
    up_shape, dn_shape = (depth, hidden), (hidden, depth)

    def both(*lead):
        return [pltpu.VMEM(lead + up_shape, bf16), pltpu.VMEM(lead + dn_shape, bf16)]

    results = (shape(tok_count, width),) * 2 + (shape(*up_shape), shape(*dn_shape))
    early = min(EARLY, experts - 1)
    made = pl.pallas_call(
        functools.partial(layer_kernel, nz, cap, SUBS, early),
        out_shape=results,
        in_specs=[HBM] * 7,
        out_specs=(VM,) * 4,
        scratch_shapes=[
            pltpu.VMEM((2, tok_count), i32),
            pltpu.VMEM((2, tok_count), f32),
            pltpu.VMEM((1, experts), i32),
            pltpu.VMEM((tok_count, width), bf16),
            pltpu.VMEM((tok_count, width), bf16),
            pltpu.VMEM((width, hidden), bf16),
            pltpu.VMEM((hidden, width), bf16),
            stage,
        ]
        + [pltpu.VMEM((flat, LANES), bf16)] * 8
        + both() + both(ny, 2) + both(ny) + both(ny) + both(2) + both(2) + both() + both(half)
        + [
            dma((7,)), dma((4,)), dma((4,)), dma((8,)), dma((8,)),
            dma((2, half, SUBS)), dma((2, half, SUBS)),
        ],
        compiler_params=pltpu.CompilerParams(
            collective_id=0, has_side_effects=True, vmem_limit_bytes=LAYER_VMEM
        ),
        name="layer",
    )(
        *(
            pltpu.with_memory_space_constraint(array, pltpu.HBM)
            for array in (
                expert_ids.T, gates.T, expert_home.reshape(1, experts), tokens, cotangent,
                up_weight.reshape(width, hidden), down_weight.reshape(hidden, width),
            )
        )
    )
    layer_out, grad_tokens, fup, fdn = pl.pallas_call(
        hand_on_kernel,
        out_shape=results,
        in_specs=[VM] * 4,
        out_specs=(HBM,) * 4,
        scratch_shapes=[dma((4,))],
        compiler_params=pltpu.CompilerParams(vmem_limit_bytes=HAND_VMEM),
        name="hand_on",
    )(*made)
    return layer_out, grad_tokens, fup[None], fdn[None]


def solution(mesh):
    rows = P(("dp", "expert"), None)
    held = P("expert", None, None)
    return jax.shard_map(
        functools.partial(local, mesh.shape["expert"] // NX, mesh.shape["dp"]),
        mesh=mesh,
        in_specs=(rows, rows, rows, rows, P(), held, held),
        out_specs=(rows, rows, P("expert", "dp", None), P("expert", None, "dp")),
        check_vma=False,
    )
```
